32 devices in a mesh: shard: 8 (over z, y), rep: 4 (over x, core).
Axes of the slice: x: 2, y: 2, z: 4, core: 2. Of those that a mesh axis runs over, the one named last changes fastest.
Arguments:
- block_input: bfloat16 [4096, 1024], P(('shard', 'rep')), may hold values from -6 to 6
- out_cotangent: bfloat16 [4096, 1024], P(('shard', 'rep')), may hold values from -6 to 6
- w_query: bfloat16 [1024, 1024], P('shard'), may hold values from -0.1875 to 0.1875
- w_key: bfloat16 [1024, 1024], P('shard'), may hold values from -0.1875 to 0.1875
- w_value: bfloat16 [1024, 1024], P('shard'), may hold values from -0.1875 to 0.1875
- w_output: bfloat16 [1024, 1024], P('shard'), may hold values from -0.75 to 0.75
- bias_query: float32 [1024], P('shard'), may hold values from -3 to 3
- bias_value: float32 [1024], P('shard'), may hold values from -3 to 3
- bias_output: float32 [1024], P('shard'), may hold values from -3 to 3
- gain_first: float32 [1024], P('shard'), may hold values from 0.5 to 1.5
- shift_first: float32 [1024], P('shard'), may hold values from -3 to 3
- w_inner: bfloat16 [1024, 4096], P('shard'), may hold values from -0.1875 to 0.1875
- bias_inner: float32 [4096], P('shard'), may hold values from -3 to 3
- w_down: bfloat16 [4096, 1024], P('shard'), may hold values from -0.09375 to 0.09375
- bias_down: float32 [1024], P('shard'), may hold values from -3 to 3
- gain_second: float32 [1024], P('shard'), may hold values from 0.5 to 1.5
- shift_second: float32 [1024], P('shard'), may hold values from -3 to 3
Outputs:
- block_output: bfloat16 [4096, 1024], P(('shard', 'rep'))
- grad_input: bfloat16 [4096, 1024], P(('shard', 'rep'))
- grad_w_query: float32 [1024, 1024], P('shard')
- grad_w_key: float32 [1024, 1024], P('shard')
- grad_w_value: float32 [1024, 1024], P('shard')
- grad_w_output: float32 [1024, 1024], P('shard')
- grad_bias_query: float32 [1024], P('shard')
- grad_bias_value: float32 [1024], P('shard')
- grad_bias_output: float32 [1024], P('shard')
- grad_gain_first: float32 [1024], P('shard')
- grad_shift_first: float32 [1024], P('shard')
- grad_w_inner: float32 [1024, 4096], P('shard')
- grad_bias_inner: float32 [4096], P('shard')
- grad_w_down: float32 [4096, 1024], P('shard')
- grad_bias_down: float32 [1024], P('shard')
- grad_gain_second: float32 [1024], P('shard')
- grad_shift_second: float32 [1024], P('shard')
The draws below stay inside these ranges and needn't reach their ends.
All inputs are finite; a program needn't handle non-finite values.
Results may differ from the reference program's by a relative error of at most 0.025.
Values may be sent and summed in bfloat16 or wider, within the bound.
A program may use at most 192 MiB of HBM per device.

```python
import math
import jax
import jax.numpy as jnp
from jax import lax

D = 1024
FF = 4096
HEADS = 16
HEAD_DIM = 64
SEQ = 128
TOKENS = 4096


def draw_block_input(key, part):
    values = jnp.clip(jax.random.normal(key, (TOKENS, D), jnp.float32), -6.0, 6.0)
    return values.astype(jnp.bfloat16)


def levels(key, dims, pieces, least, top_value):
    def one(position, parts):
        steps = jax.random.uniform(jax.random.fold_in(jax.random.fold_in(key, 6), position), (parts,), jnp.float32, least / len(pieces), top_value / len(pieces))
        return jnp.repeat(jnp.exp(steps), dims[position] // parts).reshape((-1,) + (1,) * (len(dims) - position - 1))

    level = one(*pieces[0])
    for cut in pieces[1:]:
        level = level * one(*cut)
    return level


def scatter_about(key, extent, deviation, most, shards=(), dtype=jnp.bfloat16):
    gain = levels(key, extent, shards, -0.22, 0.18) if shards else 1.0
    result = jax.random.normal(key, extent, jnp.float32) * deviation * gain
    return jnp.minimum(jnp.maximum(result, -most), most).astype(dtype)


def setup_inputs(seed: int = 0) -> dict:
    seeds = jax.random.split(jax.random.key(seed), 18)
    block_input = draw_block_input(jax.random.fold_in(seeds[17], 71), 0)
    out_cotangent = scatter_about(seeds[1], (TOKENS, D), 1.0, 6.0, ((0, 32),))
    w_query = scatter_about(seeds[2], (D, D), D ** -0.5, 0.1875, ((0, 8),))
    w_key = scatter_about(seeds[3], (D, D), D ** -0.5, 0.1875, ((0, 8),))
    w_value = scatter_about(seeds[4], (D, D), D ** -0.5, 0.1875, ((0, 8),))
    w_output = scatter_about(seeds[5], (D, D), (D // 16) ** -0.5, 0.75, ((0, 8),))
    bias_query = scatter_about(seeds[6], (D,), 0.5, 3.0, ((0, 8),), jnp.float32)
    bias_value = scatter_about(seeds[7], (D,), 0.5, 3.0, ((0, 8),), jnp.float32)
    bias_output = scatter_about(seeds[8], (D,), 0.5, 3.0, ((0, 8),), jnp.float32)
    gain_first = jnp.clip(1.0 + 0.1 * jax.random.normal(seeds[9], (D,), jnp.float32), 0.5, 1.5)
    shift_first = scatter_about(seeds[10], (D,), 0.5, 3.0, ((0, 8),), jnp.float32)
    w_inner = scatter_about(seeds[11], (D, FF), D ** -0.5, 0.1875, ((0, 8),))
    bias_inner = scatter_about(seeds[12], (FF,), 0.5, 3.0, ((0, 8),), jnp.float32)
    w_down = scatter_about(seeds[13], (FF, D), FF ** -0.5, 0.09375, ((0, 8),))
    bias_down = scatter_about(seeds[14], (D,), 0.5, 3.0, ((0, 8),), jnp.float32)
    gain_second = jnp.clip(1.0 + 0.1 * jax.random.normal(seeds[15], (D,), jnp.float32), 0.5, 1.5)
    shift_second = scatter_about(seeds[16], (D,), 0.5, 3.0, ((0, 8),), jnp.float32)
    return dict(block_input=block_input, out_cotangent=out_cotangent, w_query=w_query, w_key=w_key, w_value=w_value, w_output=w_output, bias_query=bias_query, bias_value=bias_value, bias_output=bias_output, gain_first=gain_first, shift_first=shift_first, w_inner=w_inner, bias_inner=bias_inner, w_down=w_down, bias_down=bias_down, gain_second=gain_second, shift_second=shift_second)


EPS = 1e-06
INV_ROOT_TWO = 0.7071067811865476
INV_ROOT_TWO_PI = 0.3989422804014327

def norm_parts(resid):
    centre = resid - lax.optimization_barrier(jnp.mean(resid, axis=-1, keepdims=True))
    variance = lax.optimization_barrier(jnp.mean(centre * centre, axis=-1, keepdims=True))
    rstd = lax.rsqrt(variance + EPS)
    return (centre * rstd, rstd)

def norm_back(upstream, normed, rstd):
    return rstd * (upstream - lax.optimization_barrier(jnp.mean(upstream, axis=-1, keepdims=True)) - normed * lax.optimization_barrier(jnp.mean(upstream * normed, axis=-1, keepdims=True)))

def gelu_value(inner):
    return 0.5 * inner * (1.0 + lax.erf(inner * INV_ROOT_TWO))

def gelu_slope(inner):
    return 0.5 * (1.0 + lax.erf(inner * INV_ROOT_TWO)) + inner * jnp.exp(-0.5 * inner * inner) * INV_ROOT_TWO_PI

def score_table(query4, keyed4):
    return jnp.einsum('bqhe,bkhe->bhqk', query4.astype(jnp.float32), keyed4.astype(jnp.float32)) * 0.125

def layer_pass(inputs, cotan, params):
    w_query, w_key, w_value, w_output, bias_query, bias_value, bias_output, gain_first, shift_first, w_inner, bias_inner, w_down, bias_down, gain_second, shift_second = params
    rows = inputs.shape[0]
    shape4 = (rows // SEQ, SEQ, HEADS, HEAD_DIM)
    query = (jnp.dot(inputs, w_query, preferred_element_type=jnp.float32) + bias_query).astype(jnp.bfloat16)
    keyed = jnp.dot(inputs, w_key, preferred_element_type=jnp.float32).astype(jnp.bfloat16)
    valued = (jnp.dot(inputs, w_value, preferred_element_type=jnp.float32) + bias_value).astype(jnp.bfloat16)
    query4 = query.reshape(shape4)
    keyed4 = keyed.reshape(shape4)
    valued4 = valued.reshape(shape4)
    scores = score_table(query4, keyed4)
    top = lax.optimization_barrier(jnp.max(scores, axis=-1, keepdims=True))
    logsum = top + jnp.log(lax.optimization_barrier(jnp.sum(jnp.exp(scores - top), axis=-1, keepdims=True)))
    probs_b = jnp.exp(scores - logsum).astype(jnp.bfloat16)
    context4 = jnp.einsum('bhqk,bkhe->bqhe', probs_b.astype(jnp.float32), valued4.astype(jnp.float32)).astype(jnp.bfloat16)
    context = context4.reshape(rows, D)
    resid_one = inputs.astype(jnp.float32) + jnp.dot(context, w_output, preferred_element_type=jnp.float32) + bias_output
    normed_one, rstd_one = norm_parts(resid_one)
    hidden = normed_one * gain_first + shift_first
    hidden_b = hidden.astype(jnp.bfloat16)
    inner = jnp.dot(hidden_b, w_inner, preferred_element_type=jnp.float32) + bias_inner
    acted = gelu_value(inner).astype(jnp.bfloat16)
    resid_two = hidden + jnp.dot(acted, w_down, preferred_element_type=jnp.float32) + bias_down
    normed_two, rstd_two = norm_parts(resid_two)
    output = (normed_two * gain_second + shift_second).astype(jnp.bfloat16)
    dout = cotan.astype(jnp.float32)
    g_gain_second = lax.optimization_barrier(jnp.sum(dout * normed_two, axis=0))
    g_shift_second = lax.optimization_barrier(jnp.sum(dout, axis=0))
    d_two = norm_back(dout * gain_second, normed_two, rstd_two)
    d_two_b = d_two.astype(jnp.bfloat16)
    g_bias_down = lax.optimization_barrier(jnp.sum(d_two, axis=0))
    g_w_down = jnp.dot(acted.T, d_two_b, preferred_element_type=jnp.float32)
    d_inner = jnp.dot(d_two_b, w_down.T, preferred_element_type=jnp.float32) * gelu_slope(inner)
    g_bias_inner = lax.optimization_barrier(jnp.sum(d_inner, axis=0))
    d_inner_b = d_inner.astype(jnp.bfloat16)
    g_w_inner = jnp.dot(hidden_b.T, d_inner_b, preferred_element_type=jnp.float32)
    d_hidden = d_two + jnp.dot(d_inner_b, w_inner.T, preferred_element_type=jnp.float32)
    g_gain_first = lax.optimization_barrier(jnp.sum(d_hidden * normed_one, axis=0))
    g_shift_first = lax.optimization_barrier(jnp.sum(d_hidden, axis=0))
    d_one = norm_back(d_hidden * gain_first, normed_one, rstd_one)
    g_bias_output = lax.optimization_barrier(jnp.sum(d_one, axis=0))
    d_one_b = d_one.astype(jnp.bfloat16)
    g_w_output = jnp.dot(context.T, d_one_b, preferred_element_type=jnp.float32)
    d_context = jnp.dot(d_one_b, w_output.T, preferred_element_type=jnp.float32).astype(jnp.bfloat16)
    d_context4 = d_context.reshape(shape4).astype(jnp.float32)
    probs = jnp.exp(score_table(query4, keyed4) - logsum)
    probs_again = probs.astype(jnp.bfloat16)
    d_probs = jnp.einsum('bqhe,bkhe->bhqk', d_context4, valued4.astype(jnp.float32))
    delta = lax.optimization_barrier(jnp.sum(probs * d_probs, axis=-1, keepdims=True))
    d_scores = (probs * (d_probs - delta) * 0.125).astype(jnp.bfloat16).astype(jnp.float32)
    d_query = jnp.einsum('bhqk,bkhe->bqhe', d_scores, keyed4.astype(jnp.float32)).reshape(rows, D)
    d_keyed = jnp.einsum('bhqk,bqhe->bkhe', d_scores, query4.astype(jnp.float32)).reshape(rows, D)
    d_valued = jnp.einsum('bhqk,bqhe->bkhe', probs_again.astype(jnp.float32), d_context4).reshape(rows, D)
    g_bias_query = lax.optimization_barrier(jnp.sum(d_query, axis=0))
    g_bias_value = lax.optimization_barrier(jnp.sum(d_valued, axis=0))
    dq_b = d_query.astype(jnp.bfloat16)
    dk_b = d_keyed.astype(jnp.bfloat16)
    dv_b = d_valued.astype(jnp.bfloat16)
    g_w_query = jnp.dot(inputs.T, dq_b, preferred_element_type=jnp.float32)
    g_w_key = jnp.dot(inputs.T, dk_b, preferred_element_type=jnp.float32)
    g_w_value = jnp.dot(inputs.T, dv_b, preferred_element_type=jnp.float32)
    d_input = d_one + jnp.dot(dq_b, w_query.T, preferred_element_type=jnp.float32)
    d_input = d_input + jnp.dot(dk_b, w_key.T, preferred_element_type=jnp.float32)
    d_input = d_input + jnp.dot(dv_b, w_value.T, preferred_element_type=jnp.float32)
    grads = (g_w_query, g_w_key, g_w_value, g_w_output, g_bias_query, g_bias_value, g_bias_output, g_gain_first, g_shift_first, g_w_inner, g_bias_inner, g_w_down, g_bias_down, g_gain_second, g_shift_second)
    return (output, d_input.astype(jnp.bfloat16), grads)

def reference(block_input, out_cotangent, w_query, w_key, w_value, w_output, bias_query, bias_value, bias_output, gain_first, shift_first, w_inner, bias_inner, w_down, bias_down, gain_second, shift_second):
    params = (w_query, w_key, w_value, w_output, bias_query, bias_value, bias_output, gain_first, shift_first, w_inner, bias_inner, w_down, bias_down, gain_second, shift_second)
    block_rows = math.gcd(TOKENS, 4096)
    blocks = TOKENS // block_rows
    inputs = block_input.reshape(blocks, block_rows, D)
    cotans = out_cotangent.reshape(blocks, block_rows, D)
    zeros = tuple((jnp.zeros(p.shape, jnp.float32) for p in params))

    def advance(carry, pair):
        output, d_input, grads = layer_pass(pair[0], pair[1], params)
        return (tuple((c + g for c, g in zip(carry, grads))), (output, d_input))
    totals, (outputs, d_inputs) = lax.scan(advance, zeros, (inputs, cotans))
    return (outputs.reshape(TOKENS, D), d_inputs.reshape(TOKENS, D), totals[0], totals[1], totals[2], totals[3], totals[4], totals[5], totals[6], totals[7], totals[8], totals[9], totals[10], totals[11], totals[12], totals[13], totals[14])
```

```python
import jax
import jax.numpy as jnp
from jax import lax
from jax.sharding import PartitionSpec as P

HEAD_DIM = 64
SEQ = 128
PAD = 16


EPS = 1e-06
INV_ROOT_TWO = 0.7071067811865476
INV_ROOT_TWO_PI = 0.3989422804014327
BF = jnp.bfloat16
F32 = jnp.float32


def norm_parts(resid):
    centre = resid - jnp.mean(resid, axis=-1, keepdims=True)
    variance = jnp.mean(centre * centre, axis=-1, keepdims=True)
    rstd = lax.rsqrt(variance + EPS)
    return (centre * rstd, rstd)


def norm_back(upstream, normed, rstd):
    return rstd * (
        upstream
        - jnp.mean(upstream, axis=-1, keepdims=True)
        - normed * jnp.mean(upstream * normed, axis=-1, keepdims=True)
    )


def mm(a, b):
    return jnp.dot(a, b, preferred_element_type=F32)


def mm_nt(a, b):
    return lax.dot_general(a, b, (((1,), (1,)), ((), ())), preferred_element_type=F32)


def mm_tn(a, b):
    return lax.dot_general(a, b, (((0,), (0,)), ((), ())), preferred_element_type=F32)


def ein(spec, a, b):
    return jnp.einsum(spec, a, b, preferred_element_type=F32)


def gather_rep(block):
    return lax.all_gather(block, "rep", axis=0, tiled=True)


def scatter_rep(partial):
    return lax.psum_scatter(partial, "rep", scatter_dimension=0, tiled=True).astype(F32)


def norm_one_step(partial, x, bo, gone, sone):
    resid = x.astype(F32) + scatter_rep(partial) + bo
    normed, rstd = norm_parts(resid)
    hidden = normed * gone + sone
    return normed, rstd, hidden, gather_rep(hidden.astype(BF))


def norm_two_step(partial, hidden, bd, gtwo, stwo, cot):
    normed, rstd = norm_parts(hidden + scatter_rep(partial) + bd)
    output = (normed * gtwo + stwo).astype(BF)
    dout = cot.astype(F32)
    d_two = norm_back(dout * gtwo, normed, rstd)
    sums = (jnp.sum(d_two, 0), jnp.sum(dout * normed, 0), jnp.sum(dout, 0))
    return output, d_two, sums, gather_rep(d_two.astype(BF))


def back_one_step(partial, d_two, normed, rstd, gone):
    d_hidden = d_two + scatter_rep(partial)
    d_one = norm_back(d_hidden * gone, normed, rstd)
    sums = (jnp.sum(d_one, 0), jnp.sum(d_hidden * normed, 0), jnp.sum(d_hidden, 0))
    return d_one, sums, gather_rep(d_one.astype(BF))


def body(
    block_input,
    out_cotangent,
    w_query,
    w_key,
    w_value,
    w_output,
    bias_query,
    bias_value,
    bias_output,
    gain_first,
    shift_first,
    w_inner,
    bias_inner,
    w_down,
    bias_down,
    gain_second,
    shift_second,
):
    S = lax.axis_size("shard")
    R = lax.axis_size("rep")
    r = lax.axis_index("rep")
    T = block_input.shape[0]
    D = w_query.shape[1]
    ds = w_query.shape[0]
    dr = D // R
    fs = w_down.shape[0]
    fr = fs // R
    W = 4 * dr

    def cols(w):
        return lax.dynamic_slice(w, (0, r * dr), (ds, dr))

    small = jnp.concatenate(
        [
            v.astype(BF)
            for v in (
                bias_query,
                bias_value,
                bias_output,
                gain_first,
                shift_first,
                bias_down,
                gain_second,
                shift_second,
                bias_inner,
            )
        ]
    )
    n_small = small.shape[0]
    small = jnp.pad(small, (0, PAD * W - n_small)).reshape(PAD, W)
    pack = jnp.concatenate(
        [jnp.concatenate([cols(w_query), cols(w_key), cols(w_value), cols(w_output)], 1), small], 0
    )
    got = lax.all_gather(pack, "shard", axis=0)
    x_all = gather_rep(block_input)
    wi_r = lax.dynamic_index_in_dim(w_inner.reshape(ds, S, R, fr), r, 2, keepdims=False)
    wi = lax.all_gather(wi_r.reshape(ds, S * fr), "shard", axis=0, tiled=True)
    wd = lax.all_gather(
        lax.dynamic_slice(w_down, (r * fr, 0), (fr, D)), "shard", axis=0, tiled=True
    )
    wqkv = got[:, :ds, : 3 * dr].reshape(D, 3 * dr)
    wo = lax.all_to_all(
        got[:, :ds, 3 * dr :].reshape(D, dr), "rep", split_axis=0, concat_axis=1, tiled=True
    )
    flat = got[:, ds:, :].reshape(S, PAD * W)[:, :n_small].astype(F32)
    bq, bv, bo, gone, sone, bd, gtwo, stwo = (
        flat[:, i * ds : (i + 1) * ds].reshape(D) for i in range(8)
    )
    bi = lax.dynamic_index_in_dim(flat[:, 8 * ds :].reshape(S, R, fr), r, 1, keepdims=False)
    bi = bi.reshape(S * fr)
    bq = lax.dynamic_slice(bq, (r * dr,), (dr,))
    bv = lax.dynamic_slice(bv, (r * dr,), (dr,))

    N = R * T
    shape4 = (N // SEQ, SEQ, dr // HEAD_DIM, HEAD_DIM)
    qkv = mm(x_all, wqkv)
    query = (qkv[:, :dr] + bq).astype(BF).reshape(shape4)
    keyed = qkv[:, dr : 2 * dr].astype(BF).reshape(shape4)
    valued = (qkv[:, 2 * dr :] + bv).astype(BF).reshape(shape4)
    scores = ein("bqhe,bkhe->bhqk", query, keyed) * 0.125
    top = jnp.max(scores, axis=-1, keepdims=True)
    logsum = top + jnp.log(jnp.sum(jnp.exp(scores - top), axis=-1, keepdims=True))
    probs = jnp.exp(scores - logsum)
    probs_b = probs.astype(BF)
    context = ein("bhqk,bkhe->bqhe", probs_b, valued).astype(BF).reshape(N, dr)
    attn_part = mm(context, wo).astype(BF)

    normed_one, rstd_one, hidden, hidden_all = norm_one_step(attn_part, block_input, bo, gone, sone)
    inner = mm(hidden_all, wi) + bi
    phi = 0.5 * (1.0 + lax.erf(inner * INV_ROOT_TWO))
    acted = (inner * phi).astype(BF)
    slope = phi + inner * jnp.exp(-0.5 * inner * inner) * INV_ROOT_TWO_PI
    down_part = mm(acted, wd).astype(BF)

    output, d_two, sums_two, d_two_all = norm_two_step(
        down_part, hidden, bd, gtwo, stwo, out_cotangent
    )
    d_inner = mm_nt(d_two_all, wd) * slope
    g_bias_inner = jnp.sum(d_inner, axis=0)
    d_inner_b = d_inner.astype(BF)
    hid_part = mm_nt(d_inner_b, wi).astype(BF)
    g_wd = lax.psum_scatter(
        mm_tn(acted, d_two_all).astype(BF), "shard", scatter_dimension=0, tiled=True
    )
    g_wi = lax.psum_scatter(
        mm_tn(hidden_all, d_inner_b).astype(BF), "shard", scatter_dimension=0, tiled=True
    )

    d_one, sums_one, d_one_all = back_one_step(hid_part, d_two, normed_one, rstd_one, gone)
    g_wo = mm_tn(context, d_one_all).astype(BF)
    g_wo = lax.all_to_all(g_wo, "rep", split_axis=1, concat_axis=0, tiled=True)
    d_context = mm_nt(d_one_all, wo).astype(BF).reshape(shape4)
    d_probs = ein("bqhe,bkhe->bhqk", d_context, valued)
    delta = jnp.sum(probs * d_probs, axis=-1, keepdims=True)
    d_scores = (probs * (d_probs - delta) * 0.125).astype(BF)
    d_query = ein("bhqk,bkhe->bqhe", d_scores, keyed).reshape(N, dr)
    d_keyed = ein("bhqk,bqhe->bkhe", d_scores, query).reshape(N, dr)
    d_valued = ein("bhqk,bqhe->bkhe", probs_b, d_context).reshape(N, dr)
    g_bias_query = jnp.sum(d_query, axis=0)
    g_bias_value = jnp.sum(d_valued, axis=0)
    d_qkv = jnp.concatenate([d_query.astype(BF), d_keyed.astype(BF), d_valued.astype(BF)], 1)
    in_part = mm_nt(d_qkv, wqkv).astype(BF)

    def placed(v):
        return lax.dynamic_update_slice(jnp.zeros((D,), F32), v, (r * dr,)).reshape(S, ds)

    g_small = jnp.concatenate(
        [
            placed(g_bias_query),
            placed(g_bias_value),
            sums_one[0].reshape(S, ds),
            sums_one[1].reshape(S, ds),
            sums_one[2].reshape(S, ds),
            sums_two[0].reshape(S, ds),
            sums_two[1].reshape(S, ds),
            sums_two[2].reshape(S, ds),
            g_bias_inner.reshape(S, fr),
        ],
        1,
    ).astype(BF)
    n_g = g_small.shape[1]
    g_small = jnp.pad(g_small, ((0, 0), (0, PAD * W - n_g))).reshape(S, PAD, W)
    g_pack = jnp.concatenate([mm_tn(x_all, d_qkv).astype(BF), g_wo], 1).reshape(S, ds, W)
    g_pack = jnp.concatenate([g_pack, g_small], 1)
    g_pack = lax.psum_scatter(g_pack, "shard", scatter_dimension=0, tiled=True)[0]

    grad_input = (d_one + scatter_rep(in_part)).astype(BF)

    wd_out = gather_rep(g_wd).astype(F32)
    wi_out = lax.all_gather(g_wi, "rep", axis=0).astype(F32)
    wi_out = wi_out.reshape(R, ds, S, fr).transpose(1, 2, 0, 3).reshape(ds, S * R * fr)
    packs = lax.all_gather(g_pack, "rep", axis=0).astype(F32)
    main = packs[:, :ds].reshape(R, ds, 4, dr).transpose(2, 1, 0, 3).reshape(4, ds, D)
    tail = packs[:, ds:].reshape(R, PAD * W)
    summed = jnp.sum(tail[:, : 8 * ds], axis=0)
    gbq, gbv, gbo, ggone, gsone, gbd, ggtwo, gstwo = (
        summed[i * ds : (i + 1) * ds] for i in range(8)
    )
    gbi = tail[:, 8 * ds : n_g].reshape(fs)
    return (
        output,
        grad_input,
        main[0],
        main[1],
        main[2],
        main[3],
        gbq,
        gbv,
        gbo,
        ggone,
        gsone,
        wi_out,
        gbi,
        wd_out,
        gbd,
        ggtwo,
        gstwo,
    )


def solution(mesh):
    tokens = P(("shard", "rep"), None)
    mat = P("shard", None)
    vec = P("shard")
    params = (mat, mat, mat, mat, vec, vec, vec, vec, vec, mat, vec, mat, vec, vec, vec)
    return jax.shard_map(
        body,
        mesh=mesh,
        in_specs=(tokens, tokens) + params,
        out_specs=(tokens, tokens) + params,
        check_vma=False,
    )
```

```python
import jax
import jax.numpy as jnp
from jax import lax
from jax.experimental import pallas as pl
from jax.experimental.pallas import tpu as pltpu
from jax.sharding import PartitionSpec as P

HEAD_DIM = 64
SEQ = 128
PAD = 16


EPS = 1e-06
INV_ROOT_TWO = 0.7071067811865476
INV_ROOT_TWO_PI = 0.3989422804014327
BF = jnp.bfloat16
F32 = jnp.float32


def norm_parts(resid):
    centre = resid - jnp.mean(resid, axis=-1, keepdims=True)
    variance = jnp.mean(centre * centre, axis=-1, keepdims=True)
    rstd = lax.rsqrt(variance + EPS)
    return (centre * rstd, rstd)


def norm_back(upstream, normed, rstd):
    return rstd * (
        upstream
        - jnp.mean(upstream, axis=-1, keepdims=True)
        - normed * jnp.mean(upstream * normed, axis=-1, keepdims=True)
    )


def mm(a, b):
    return jnp.dot(a, b, preferred_element_type=F32)


def mm_nt(a, b):
    return lax.dot_general(a, b, (((1,), (1,)), ((), ())), preferred_element_type=F32)


def mm_tn(a, b):
    return lax.dot_general(a, b, (((0,), (0,)), ((), ())), preferred_element_type=F32)


def ein(spec, a, b):
    return jnp.einsum(spec, a, b, preferred_element_type=F32)


def gather_rep(block):
    return lax.all_gather(block, "rep", axis=0, tiled=True)


MESH = pl.DeviceIdType.MESH
CHUNK = 16


class Peers:
    def __init__(self, R):
        self.R, self.A = R, R // 2
        self.me = lax.axis_index("rep")
        self.c = lax.rem(self.me, 2)
        self.a = lax.div(self.me, 2)
        self.partner = self.me + 1 - 2 * self.c

    def chip(self, k):
        return lax.rem(self.a + k, self.A)

    def same(self, k):
        return 2 * self.chip(k) + self.c

    def other(self, k):
        return 2 * self.chip(k) + 1 - self.c

    def meet(self):
        barrier = pltpu.get_barrier_semaphore()
        for dev in [self.partner] + [self.same(k) for k in range(1, self.A)]:
            pl.semaphore_signal(barrier, inc=1, device_id={"rep": dev}, device_id_type=MESH)
        pl.semaphore_wait(barrier, self.A)


def rows_of(index, T):
    return pl.ds(pl.multiple_of(index * T, T), T)


def chunk_rows(i, base=None):
    start = i * CHUNK if base is None else base + i * CHUNK
    return pl.ds(pl.multiple_of(start, CHUNK), CHUNK)


def remote(src, dst, send, recv, dev):
    return pltpu.make_async_remote_copy(
        src_ref=src,
        dst_ref=dst,
        send_sem=send,
        recv_sem=recv,
        device_id={"rep": dev},
        device_id_type=MESH,
    )


def scatter_sum(p, part, T, near, far, out, sems):
    near_s, near_r, far_s, far_r = sems
    order = list(range(1, p.A)) + [0]
    first = {
        k: remote(
            part.at[rows_of(p.other(k), T)], near.at[k], near_s.at[k], near_r.at[k], p.partner
        )
        for k in order
    }
    for k in order:
        first[k].start()
    second = []
    for k in range(1, p.A):
        first[k].wait_recv()
        base = p.same(k) * T

        def add(i, _, k=k, base=base):
            mine = part[chunk_rows(i, base), :].astype(F32)
            out[k - 1, chunk_rows(i), :] = (mine + near[k, chunk_rows(i), :].astype(F32)).astype(BF)
            return 0

        lax.fori_loop(0, T // CHUNK, add, 0)
        copy = remote(out.at[k - 1], far.at[k - 1], far_s.at[k - 1], far_r.at[k - 1], p.same(k))
        copy.start()
        second.append(copy)
    first[0].wait_recv()
    for copy in second:
        copy.wait_recv()

    def read(i):
        total = part[chunk_rows(i, p.me * T), :].astype(F32) + near[0, chunk_rows(i), :].astype(F32)
        for k in range(1, p.A):
            total = total + far[k - 1, chunk_rows(i), :].astype(F32)
        return total

    return read, list(first.values()) + second


def spread(p, src, full, T, sems):
    dir_s, dir_r, fwd_s, fwd_r = sems
    mine = full.at[rows_of(p.me, T)]
    direct = {}
    for k in list(range(1, p.A)) + [0]:
        dev = p.partner if k == 0 else p.same(k)
        direct[k] = remote(src, mine, dir_s.at[k], dir_r.at[k], dev)
        direct[k].start()
    passed = []
    for k in range(1, p.A):
        direct[k].wait_recv()
        block = full.at[rows_of(p.same(p.A - k), T)]
        copy = remote(block, block, fwd_s.at[k - 1], fwd_r.at[k - 1], p.partner)
        copy.start()
        passed.append(copy)
    direct[0].wait_recv()
    for copy in passed:
        copy.wait_recv()
    return list(direct.values()) + passed


def drain(copies):
    for copy in copies:
        copy.wait_send()


def run_kernel(kernel, cid, T, D, R, ins, outs, scatter, gather):
    A = R // 2
    few = max(A - 1, 1)
    scratch = []
    if scatter:
        scratch += [
            pltpu.VMEM((A, T, D), BF),
            pltpu.VMEM((few, T, D), BF),
            pltpu.VMEM((few, T, D), BF),
        ]
        scratch += [pltpu.SemaphoreType.DMA((n,)) for n in (A, A, few, few)]
    if gather:
        scratch += [pltpu.SemaphoreType.DMA((n,)) for n in (A, A, few, few)]
    vmem = pl.BlockSpec(memory_space=pltpu.VMEM)
    return pl.pallas_call(
        kernel,
        out_shape=[jax.ShapeDtypeStruct(*o) for o in outs],
        in_specs=[vmem] * len(ins),
        out_specs=[vmem] * len(outs),
        scratch_shapes=scratch,
        compiler_params=pltpu.CompilerParams(collective_id=cid, has_side_effects=True),
        cost_estimate=pl.CostEstimate(flops=0, bytes_accessed=24 << 20, transcendentals=0),
    )(*ins)


def gather_kernel(block, R, cid):
    T, D = block.shape

    def kernel(src, full, *sems):
        p = Peers(R)
        p.meet()

        def put(i, _):
            full[chunk_rows(i, p.me * T), :] = src[chunk_rows(i), :]
            return 0

        lax.fori_loop(0, T // CHUNK, put, 0)
        drain(spread(p, src, full, T, sems))

    return run_kernel(kernel, cid, T, D, R, [block], [((R * T, D), BF)], False, True)[0]


def norm_one_step(partial, x, bo, gone, sone):
    T, D = x.shape
    R = partial.shape[0] // T

    def kernel(part, xr, bor, gr, sr, normed_o, rstd_o, hidden_o, full, near, far, out, *sems):
        p = Peers(R)
        p.meet()
        read, sent = scatter_sum(p, part, T, near, far, out, sems[:4])

        def step(i, _):
            normed, rstd = norm_parts(xr[chunk_rows(i), :].astype(F32) + read(i) + bor[...])
            hidden = normed * gr[...] + sr[...]
            normed_o[chunk_rows(i), :] = normed
            rstd_o[chunk_rows(i), :] = rstd
            hidden_o[chunk_rows(i), :] = hidden
            full[chunk_rows(i, p.me * T), :] = hidden.astype(BF)
            return 0

        lax.fori_loop(0, T // CHUNK, step, 0)
        drain(sent + spread(p, full.at[rows_of(p.me, T)], full, T, sems[4:]))

    ins = [partial, x, bo[None], gone[None], sone[None]]
    outs = [((T, D), F32), ((T, 1), F32), ((T, D), F32), ((R * T, D), BF)]
    return run_kernel(kernel, 1, T, D, R, ins, outs, True, True)


def add_sums(ref, values):
    for n, v in enumerate(values):
        ref[n : n + 1, :] += jnp.sum(v, axis=0, keepdims=True)


def norm_two_step(partial, hidden, bd, gtwo, stwo, cot):
    T, D = hidden.shape
    R = partial.shape[0] // T

    def kernel(part, hr, br, gr, sr, cr, out_o, d_o, sums, full, near, far, out, *sems):
        p = Peers(R)
        p.meet()
        sums[...] = jnp.zeros_like(sums)
        read, sent = scatter_sum(p, part, T, near, far, out, sems[:4])

        def step(i, _):
            normed, rstd = norm_parts(hr[chunk_rows(i), :] + read(i) + br[...])
            out_o[chunk_rows(i), :] = (normed * gr[...] + sr[...]).astype(BF)
            dout = cr[chunk_rows(i), :].astype(F32)
            d_two = norm_back(dout * gr[...], normed, rstd)
            add_sums(sums, (d_two, dout * normed, dout))
            d_o[chunk_rows(i), :] = d_two
            full[chunk_rows(i, p.me * T), :] = d_two.astype(BF)
            return 0

        lax.fori_loop(0, T // CHUNK, step, 0)
        drain(sent + spread(p, full.at[rows_of(p.me, T)], full, T, sems[4:]))

    ins = [partial, hidden, bd[None], gtwo[None], stwo[None], cot]
    outs = [((T, D), BF), ((T, D), F32), ((8, D), F32), ((R * T, D), BF)]
    return run_kernel(kernel, 2, T, D, R, ins, outs, True, True)


def back_one_step(partial, d_two, normed, rstd, gone):
    T, D = d_two.shape
    R = partial.shape[0] // T

    def kernel(part, dr, nr, rr, gr, d_o, sums, full, near, far, out, *sems):
        p = Peers(R)
        p.meet()
        sums[...] = jnp.zeros_like(sums)
        read, sent = scatter_sum(p, part, T, near, far, out, sems[:4])

        def step(i, _):
            d_hidden = dr[chunk_rows(i), :] + read(i)
            normed = nr[chunk_rows(i), :]
            d_one = norm_back(d_hidden * gr[...], normed, rr[chunk_rows(i), :])
            add_sums(sums, (d_one, d_hidden * normed, d_hidden))
            d_o[chunk_rows(i), :] = d_one
            full[chunk_rows(i, p.me * T), :] = d_one.astype(BF)
            return 0

        lax.fori_loop(0, T // CHUNK, step, 0)
        drain(sent + spread(p, full.at[rows_of(p.me, T)], full, T, sems[4:]))

    ins = [partial, d_two, normed, rstd, gone[None]]
    outs = [((T, D), F32), ((8, D), F32), ((R * T, D), BF)]
    return run_kernel(kernel, 3, T, D, R, ins, outs, True, True)


def input_step(partial, d_one):
    T, D = d_one.shape
    R = partial.shape[0] // T

    def kernel(part, dr, grad, near, far, out, *sems):
        p = Peers(R)
        p.meet()
        read, sent = scatter_sum(p, part, T, near, far, out, sems)

        def step(i, _):
            grad[chunk_rows(i), :] = (dr[chunk_rows(i), :] + read(i)).astype(BF)
            return 0

        lax.fori_loop(0, T // CHUNK, step, 0)
        drain(sent)

    return run_kernel(kernel, 4, T, D, R, [partial, d_one], [((T, D), BF)], True, False)[0]


def body(
    block_input,
    out_cotangent,
    w_query,
    w_key,
    w_value,
    w_output,
    bias_query,
    bias_value,
    bias_output,
    gain_first,
    shift_first,
    w_inner,
    bias_inner,
    w_down,
    bias_down,
    gain_second,
    shift_second,
):
    S = lax.axis_size("shard")
    R = lax.axis_size("rep")
    r = lax.axis_index("rep")
    T = block_input.shape[0]
    D = w_query.shape[1]
    ds = w_query.shape[0]
    dr = D // R
    fs = w_down.shape[0]
    fr = fs // R
    W = 4 * dr

    def cols(w):
        return lax.dynamic_slice(w, (0, r * dr), (ds, dr))

    small = jnp.concatenate(
        [
            v.astype(BF)
            for v in (
                bias_query,
                bias_value,
                bias_output,
                gain_first,
                shift_first,
                bias_down,
                gain_second,
                shift_second,
                bias_inner,
            )
        ]
    )
    n_small = small.shape[0]
    small = jnp.pad(small, (0, PAD * W - n_small)).reshape(PAD, W)
    pack = jnp.concatenate(
        [jnp.concatenate([cols(w_query), cols(w_key), cols(w_value), cols(w_output)], 1), small], 0
    )
    got = lax.all_gather(pack, "shard", axis=0)
    x_all = gather_kernel(block_input, R, 0)
    wi_r = lax.dynamic_index_in_dim(w_inner.reshape(ds, S, R, fr), r, 2, keepdims=False)
    wi = lax.all_gather(wi_r.reshape(ds, S * fr), "shard", axis=0, tiled=True)
    wd = lax.all_gather(
        lax.dynamic_slice(w_down, (r * fr, 0), (fr, D)), "shard", axis=0, tiled=True
    )
    wqkv = got[:, :ds, : 3 * dr].reshape(D, 3 * dr)
    wo = lax.all_to_all(
        got[:, :ds, 3 * dr :].reshape(D, dr), "rep", split_axis=0, concat_axis=1, tiled=True
    )
    flat = got[:, ds:, :].reshape(S, PAD * W)[:, :n_small].astype(F32)
    bq, bv, bo, gone, sone, bd, gtwo, stwo = (
        flat[:, i * ds : (i + 1) * ds].reshape(D) for i in range(8)
    )
    bi = lax.dynamic_index_in_dim(flat[:, 8 * ds :].reshape(S, R, fr), r, 1, keepdims=False)
    bi = bi.reshape(S * fr)
    bq = lax.dynamic_slice(bq, (r * dr,), (dr,))
    bv = lax.dynamic_slice(bv, (r * dr,), (dr,))

    N = R * T
    shape4 = (N // SEQ, SEQ, dr // HEAD_DIM, HEAD_DIM)
    qkv = mm(x_all, wqkv)
    query = (qkv[:, :dr] + bq).astype(BF).reshape(shape4)
    keyed = qkv[:, dr : 2 * dr].astype(BF).reshape(shape4)
    valued = (qkv[:, 2 * dr :] + bv).astype(BF).reshape(shape4)
    scores = ein("bqhe,bkhe->bhqk", query, keyed) * 0.125
    top = jnp.max(scores, axis=-1, keepdims=True)
    logsum = top + jnp.log(jnp.sum(jnp.exp(scores - top), axis=-1, keepdims=True))
    probs = jnp.exp(scores - logsum)
    probs_b = probs.astype(BF)
    context = ein("bhqk,bkhe->bqhe", probs_b, valued).astype(BF).reshape(N, dr)
    attn_part = mm(context, wo).astype(BF)

    normed_one, rstd_one, hidden, hidden_all = norm_one_step(attn_part, block_input, bo, gone, sone)
    inner = mm(hidden_all, wi) + bi
    phi = 0.5 * (1.0 + lax.erf(inner * INV_ROOT_TWO))
    acted = (inner * phi).astype(BF)
    slope = phi + inner * jnp.exp(-0.5 * inner * inner) * INV_ROOT_TWO_PI
    down_part = mm(acted, wd).astype(BF)

    output, d_two, sums_two, d_two_all = norm_two_step(
        down_part, hidden, bd, gtwo, stwo, out_cotangent
    )
    d_inner = mm_nt(d_two_all, wd) * slope
    g_bias_inner = jnp.sum(d_inner, axis=0)
    d_inner_b = d_inner.astype(BF)
    hid_part = mm_nt(d_inner_b, wi).astype(BF)
    g_wd = lax.psum_scatter(
        mm_tn(acted, d_two_all).astype(BF), "shard", scatter_dimension=0, tiled=True
    )
    g_wi = lax.psum_scatter(
        mm_tn(hidden_all, d_inner_b).astype(BF), "shard", scatter_dimension=0, tiled=True
    )

    d_one, sums_one, d_one_all = back_one_step(hid_part, d_two, normed_one, rstd_one, gone)
    g_wo = mm_tn(context, d_one_all).astype(BF)
    g_wo = lax.all_to_all(g_wo, "rep", split_axis=1, concat_axis=0, tiled=True)
    d_context = mm_nt(d_one_all, wo).astype(BF).reshape(shape4)
    d_probs = ein("bqhe,bkhe->bhqk", d_context, valued)
    delta = jnp.sum(probs * d_probs, axis=-1, keepdims=True)
    d_scores = (probs * (d_probs - delta) * 0.125).astype(BF)
    d_query = ein("bhqk,bkhe->bqhe", d_scores, keyed).reshape(N, dr)
    d_keyed = ein("bhqk,bqhe->bkhe", d_scores, query).reshape(N, dr)
    d_valued = ein("bhqk,bqhe->bkhe", probs_b, d_context).reshape(N, dr)
    g_bias_query = jnp.sum(d_query, axis=0)
    g_bias_value = jnp.sum(d_valued, axis=0)
    d_qkv = jnp.concatenate([d_query.astype(BF), d_keyed.astype(BF), d_valued.astype(BF)], 1)
    in_part = mm_nt(d_qkv, wqkv).astype(BF)

    def placed(v):
        return lax.dynamic_update_slice(jnp.zeros((D,), F32), v, (r * dr,)).reshape(S, ds)

    g_small = jnp.concatenate(
        [
            placed(g_bias_query),
            placed(g_bias_value),
            sums_one[0].reshape(S, ds),
            sums_one[1].reshape(S, ds),
            sums_one[2].reshape(S, ds),
            sums_two[0].reshape(S, ds),
            sums_two[1].reshape(S, ds),
            sums_two[2].reshape(S, ds),
            g_bias_inner.reshape(S, fr),
        ],
        1,
    ).astype(BF)
    n_g = g_small.shape[1]
    g_small = jnp.pad(g_small, ((0, 0), (0, PAD * W - n_g))).reshape(S, PAD, W)
    g_pack = jnp.concatenate([mm_tn(x_all, d_qkv).astype(BF), g_wo], 1).reshape(S, ds, W)
    g_pack = jnp.concatenate([g_pack, g_small], 1)
    g_pack = lax.psum_scatter(g_pack, "shard", scatter_dimension=0, tiled=True)[0]

    grad_input = input_step(in_part, d_one)

    wd_out = gather_rep(g_wd).astype(F32)
    wi_out = lax.all_gather(g_wi, "rep", axis=0).astype(F32)
    wi_out = wi_out.reshape(R, ds, S, fr).transpose(1, 2, 0, 3).reshape(ds, S * R * fr)
    packs = lax.all_gather(g_pack, "rep", axis=0).astype(F32)
    main = packs[:, :ds].reshape(R, ds, 4, dr).transpose(2, 1, 0, 3).reshape(4, ds, D)
    tail = packs[:, ds:].reshape(R, PAD * W)
    summed = jnp.sum(tail[:, : 8 * ds], axis=0)
    gbq, gbv, gbo, ggone, gsone, gbd, ggtwo, gstwo = (
        summed[i * ds : (i + 1) * ds] for i in range(8)
    )
    gbi = tail[:, 8 * ds : n_g].reshape(fs)
    return (
        output,
        grad_input,
        main[0],
        main[1],
        main[2],
        main[3],
        gbq,
        gbv,
        gbo,
        ggone,
        gsone,
        wi_out,
        gbi,
        wd_out,
        gbd,
        ggtwo,
        gstwo,
    )


def solution(mesh):
    tokens = P(("shard", "rep"), None)
    mat = P("shard", None)
    vec = P("shard")
    params = (mat, mat, mat, mat, vec, vec, vec, vec, vec, mat, vec, mat, vec, vec, vec)
    return jax.shard_map(
        body,
        mesh=mesh,
        in_specs=(tokens, tokens) + params,
        out_specs=(tokens, tokens) + params,
        check_vma=False,
    )
```

```python
import jax
import jax.numpy as jnp
from jax import lax
from jax.experimental import pallas as pl
from jax.experimental.pallas import tpu as pltpu
from jax.sharding import PartitionSpec as P

HEAD_DIM = 64
SEQ = 128
PAD = 16


EPS = 1e-06
INV_ROOT_TWO = 0.7071067811865476
INV_ROOT_TWO_PI = 0.3989422804014327
BF = jnp.bfloat16
F32 = jnp.float32


def norm_parts(resid):
    centre = resid - jnp.mean(resid, axis=-1, keepdims=True)
    variance = jnp.mean(centre * centre, axis=-1, keepdims=True)
    rstd = lax.rsqrt(variance + EPS)
    return (centre * rstd, rstd)


def norm_back(upstream, normed, rstd):
    return rstd * (
        upstream
        - jnp.mean(upstream, axis=-1, keepdims=True)
        - normed * jnp.mean(upstream * normed, axis=-1, keepdims=True)
    )


def mm(a, b):
    return jnp.dot(a, b, preferred_element_type=F32)


def mm_nt(a, b):
    return lax.dot_general(a, b, (((1,), (1,)), ((), ())), preferred_element_type=F32)


def mm_tn(a, b):
    return lax.dot_general(a, b, (((0,), (0,)), ((), ())), preferred_element_type=F32)


def ein(spec, a, b):
    return jnp.einsum(spec, a, b, preferred_element_type=F32)


MESH = pl.DeviceIdType.MESH
CHUNK = 16


class Peers:
    def __init__(self, R):
        self.R, self.A = R, R // 2
        self.me = lax.axis_index("rep")
        self.c = lax.rem(self.me, 2)
        self.a = lax.div(self.me, 2)
        self.partner = self.me + 1 - 2 * self.c

    def chip(self, k):
        return lax.rem(self.a + k, self.A)

    def same(self, k):
        return 2 * self.chip(k) + self.c

    def other(self, k):
        return 2 * self.chip(k) + 1 - self.c

    def meet(self):
        barrier = pltpu.get_barrier_semaphore()
        for dev in [self.partner] + [self.same(k) for k in range(1, self.A)]:
            pl.semaphore_signal(barrier, inc=1, device_id={"rep": dev}, device_id_type=MESH)
        pl.semaphore_wait(barrier, self.A)


def rows_of(index, T):
    return pl.ds(pl.multiple_of(index * T, T), T)


def chunk_rows(i, base=None):
    start = i * CHUNK if base is None else base + i * CHUNK
    return pl.ds(pl.multiple_of(start, CHUNK), CHUNK)


def remote(src, dst, send, recv, dev):
    return pltpu.make_async_remote_copy(
        src_ref=src,
        dst_ref=dst,
        send_sem=send,
        recv_sem=recv,
        device_id={"rep": dev},
        device_id_type=MESH,
    )


def scatter_sum(p, part, T, near, far, out, sems):
    near_s, near_r, far_s, far_r = sems
    order = list(range(1, p.A)) + [0]
    first = {
        k: remote(
            part.at[rows_of(p.other(k), T)], near.at[k], near_s.at[k], near_r.at[k], p.partner
        )
        for k in order
    }
    for k in order:
        first[k].start()
    second = []
    for k in range(1, p.A):
        first[k].wait_recv()
        base = p.same(k) * T

        def add(i, _, k=k, base=base):
            mine = part[chunk_rows(i, base), :].astype(F32)
            out[k - 1, chunk_rows(i), :] = (mine + near[k, chunk_rows(i), :].astype(F32)).astype(BF)
            return 0

        lax.fori_loop(0, T // CHUNK, add, 0)
        copy = remote(out.at[k - 1], far.at[k - 1], far_s.at[k - 1], far_r.at[k - 1], p.same(k))
        copy.start()
        second.append(copy)
    first[0].wait_recv()
    for copy in second:
        copy.wait_recv()

    def read(i):
        total = part[chunk_rows(i, p.me * T), :].astype(F32) + near[0, chunk_rows(i), :].astype(F32)
        for k in range(1, p.A):
            total = total + far[k - 1, chunk_rows(i), :].astype(F32)
        return total

    return read, list(first.values()) + second


def spread(p, src, full, T, sems):
    dir_s, dir_r, fwd_s, fwd_r = sems
    mine = full.at[rows_of(p.me, T)]
    direct = {}
    for k in list(range(1, p.A)) + [0]:
        dev = p.partner if k == 0 else p.same(k)
        direct[k] = remote(src, mine, dir_s.at[k], dir_r.at[k], dev)
        direct[k].start()
    passed = []
    for k in range(1, p.A):
        direct[k].wait_recv()
        block = full.at[rows_of(p.same(p.A - k), T)]
        copy = remote(block, block, fwd_s.at[k - 1], fwd_r.at[k - 1], p.partner)
        copy.start()
        passed.append(copy)
    direct[0].wait_recv()
    for copy in passed:
        copy.wait_recv()
    return list(direct.values()) + passed


def drain(copies):
    for copy in copies:
        copy.wait_send()


def run_kernel(kernel, cid, T, D, R, ins, outs, scatter, gather):
    A = R // 2
    few = max(A - 1, 1)
    scratch = []
    if scatter:
        scratch += [
            pltpu.VMEM((A, T, D), BF),
            pltpu.VMEM((few, T, D), BF),
            pltpu.VMEM((few, T, D), BF),
        ]
        scratch += [pltpu.SemaphoreType.DMA((n,)) for n in (A, A, few, few)]
    if gather:
        scratch += [pltpu.SemaphoreType.DMA((n,)) for n in (A, A, few, few)]
    vmem = pl.BlockSpec(memory_space=pltpu.VMEM)
    return pl.pallas_call(
        kernel,
        out_shape=[jax.ShapeDtypeStruct(*o) for o in outs],
        in_specs=[vmem] * len(ins),
        out_specs=[vmem] * len(outs),
        scratch_shapes=scratch,
        compiler_params=pltpu.CompilerParams(collective_id=cid, has_side_effects=True),
        cost_estimate=pl.CostEstimate(flops=0, bytes_accessed=24 << 20, transcendentals=0),
    )(*ins)


def gather_kernel(block, R, cid):
    T, D = block.shape

    def kernel(src, full, *sems):
        p = Peers(R)
        p.meet()

        def put(i, _):
            full[chunk_rows(i, p.me * T), :] = src[chunk_rows(i), :]
            return 0

        lax.fori_loop(0, T // CHUNK, put, 0)
        drain(spread(p, src, full, T, sems))

    return run_kernel(kernel, cid, T, D, R, [block], [((R * T, D), BF)], False, True)[0]


def norm_one_step(partial, x, bo, gone, sone):
    T, D = x.shape
    R = partial.shape[0] // T

    def kernel(part, xr, bor, gr, sr, normed_o, rstd_o, hidden_o, full, near, far, out, *sems):
        p = Peers(R)
        p.meet()
        read, sent = scatter_sum(p, part, T, near, far, out, sems[:4])

        def step(i, _):
            normed, rstd = norm_parts(xr[chunk_rows(i), :].astype(F32) + read(i) + bor[...])
            hidden = normed * gr[...] + sr[...]
            normed_o[chunk_rows(i), :] = normed
            rstd_o[chunk_rows(i), :] = rstd
            hidden_o[chunk_rows(i), :] = hidden
            full[chunk_rows(i, p.me * T), :] = hidden.astype(BF)
            return 0

        lax.fori_loop(0, T // CHUNK, step, 0)
        drain(sent + spread(p, full.at[rows_of(p.me, T)], full, T, sems[4:]))

    ins = [partial, x, bo[None], gone[None], sone[None]]
    outs = [((T, D), F32), ((T, 1), F32), ((T, D), F32), ((R * T, D), BF)]
    return run_kernel(kernel, 1, T, D, R, ins, outs, True, True)


def add_sums(ref, values):
    for n, v in enumerate(values):
        ref[n : n + 1, :] += jnp.sum(v, axis=0, keepdims=True)


def norm_two_step(partial, hidden, bd, gtwo, stwo, cot):
    T, D = hidden.shape
    R = partial.shape[0] // T

    def kernel(part, hr, br, gr, sr, cr, out_o, d_o, sums, full, near, far, out, *sems):
        p = Peers(R)
        p.meet()
        sums[...] = jnp.zeros_like(sums)
        read, sent = scatter_sum(p, part, T, near, far, out, sems[:4])

        def step(i, _):
            normed, rstd = norm_parts(hr[chunk_rows(i), :] + read(i) + br[...])
            out_o[chunk_rows(i), :] = (normed * gr[...] + sr[...]).astype(BF)
            dout = cr[chunk_rows(i), :].astype(F32)
            d_two = norm_back(dout * gr[...], normed, rstd)
            add_sums(sums, (d_two, dout * normed, dout))
            d_o[chunk_rows(i), :] = d_two
            full[chunk_rows(i, p.me * T), :] = d_two.astype(BF)
            return 0

        lax.fori_loop(0, T // CHUNK, step, 0)
        drain(sent + spread(p, full.at[rows_of(p.me, T)], full, T, sems[4:]))

    ins = [partial, hidden, bd[None], gtwo[None], stwo[None], cot]
    outs = [((T, D), BF), ((T, D), F32), ((8, D), F32), ((R * T, D), BF)]
    return run_kernel(kernel, 2, T, D, R, ins, outs, True, True)


def back_one_step(partial, d_two, normed, rstd, gone):
    T, D = d_two.shape
    R = partial.shape[0] // T

    def kernel(part, dr, nr, rr, gr, d_o, sums, full, near, far, out, *sems):
        p = Peers(R)
        p.meet()
        sums[...] = jnp.zeros_like(sums)
        read, sent = scatter_sum(p, part, T, near, far, out, sems[:4])

        def step(i, _):
            d_hidden = dr[chunk_rows(i), :] + read(i)
            normed = nr[chunk_rows(i), :]
            d_one = norm_back(d_hidden * gr[...], normed, rr[chunk_rows(i), :])
            add_sums(sums, (d_one, d_hidden * normed, d_hidden))
            d_o[chunk_rows(i), :] = d_one
            full[chunk_rows(i, p.me * T), :] = d_one.astype(BF)
            return 0

        lax.fori_loop(0, T // CHUNK, step, 0)
        drain(sent + spread(p, full.at[rows_of(p.me, T)], full, T, sems[4:]))

    ins = [partial, d_two, normed, rstd, gone[None]]
    outs = [((T, D), F32), ((8, D), F32), ((R * T, D), BF)]
    return run_kernel(kernel, 3, T, D, R, ins, outs, True, True)


def input_step(partial, d_one):
    T, D = d_one.shape
    R = partial.shape[0] // T

    def kernel(part, dr, grad, near, far, out, *sems):
        p = Peers(R)
        p.meet()
        read, sent = scatter_sum(p, part, T, near, far, out, sems)

        def step(i, _):
            grad[chunk_rows(i), :] = (dr[chunk_rows(i), :] + read(i)).astype(BF)
            return 0

        lax.fori_loop(0, T // CHUNK, step, 0)
        drain(sent)

    return run_kernel(kernel, 4, T, D, R, [partial, d_one], [((T, D), BF)], True, False)[0]


def body(
    block_input,
    out_cotangent,
    w_query,
    w_key,
    w_value,
    w_output,
    bias_query,
    bias_value,
    bias_output,
    gain_first,
    shift_first,
    w_inner,
    bias_inner,
    w_down,
    bias_down,
    gain_second,
    shift_second,
):
    S = lax.axis_size("shard")
    R = lax.axis_size("rep")
    r = lax.axis_index("rep")
    T = block_input.shape[0]
    D = w_query.shape[1]
    ds = w_query.shape[0]
    dr = D // R
    fs = w_down.shape[0]
    fr = fs // R
    W = 4 * dr

    def cols(w):
        return lax.dynamic_slice(w, (0, r * dr), (ds, dr))

    small = jnp.concatenate(
        [
            v.astype(BF)
            for v in (
                bias_query,
                bias_value,
                bias_output,
                gain_first,
                shift_first,
                bias_down,
                gain_second,
                shift_second,
                bias_inner,
            )
        ]
    )
    n_small = small.shape[0]
    small = jnp.pad(small, (0, PAD * W - n_small)).reshape(PAD, W)
    pack = jnp.concatenate(
        [jnp.concatenate([cols(w_query), cols(w_key), cols(w_value), cols(w_output)], 1), small], 0
    )
    got = lax.all_gather(pack, "shard", axis=0)
    x_all = gather_kernel(block_input, R, 0)
    wi_r = lax.dynamic_index_in_dim(w_inner.reshape(ds, S, R, fr), r, 2, keepdims=False)
    V = S * fr
    dv = fr * D // V
    wd_r = lax.dynamic_slice(w_down, (r * fr, 0), (fr, D)).reshape(dv, V)
    mlp = lax.all_gather(jnp.concatenate([wi_r.reshape(ds, V), wd_r], 0), "shard", axis=0)
    wi = mlp[:, :ds].reshape(D, V)
    wd = mlp[:, ds:].reshape(V, D)
    wqkv = got[:, :ds, : 3 * dr].reshape(D, 3 * dr)
    wo = lax.all_to_all(
        got[:, :ds, 3 * dr :].reshape(D, dr), "rep", split_axis=0, concat_axis=1, tiled=True
    )
    flat = got[:, ds:, :].reshape(S, PAD * W)[:, :n_small].astype(F32)
    bq, bv, bo, gone, sone, bd, gtwo, stwo = (
        flat[:, i * ds : (i + 1) * ds].reshape(D) for i in range(8)
    )
    bi = lax.dynamic_index_in_dim(flat[:, 8 * ds :].reshape(S, R, fr), r, 1, keepdims=False)
    bi = bi.reshape(S * fr)
    bq = lax.dynamic_slice(bq, (r * dr,), (dr,))
    bv = lax.dynamic_slice(bv, (r * dr,), (dr,))

    N = R * T
    shape4 = (N // SEQ, SEQ, dr // HEAD_DIM, HEAD_DIM)
    qkv = mm(x_all, wqkv)
    query = (qkv[:, :dr] + bq).astype(BF).reshape(shape4)
    keyed = qkv[:, dr : 2 * dr].astype(BF).reshape(shape4)
    valued = (qkv[:, 2 * dr :] + bv).astype(BF).reshape(shape4)
    scores = ein("bqhe,bkhe->bhqk", query, keyed) * 0.125
    top = jnp.max(scores, axis=-1, keepdims=True)
    logsum = top + jnp.log(jnp.sum(jnp.exp(scores - top), axis=-1, keepdims=True))
    probs = jnp.exp(scores - logsum)
    probs_b = probs.astype(BF)
    context = ein("bhqk,bkhe->bqhe", probs_b, valued).astype(BF).reshape(N, dr)
    attn_part = mm(context, wo).astype(BF)

    normed_one, rstd_one, hidden, hidden_all = norm_one_step(attn_part, block_input, bo, gone, sone)
    inner = mm(hidden_all, wi) + bi
    phi = 0.5 * (1.0 + lax.erf(inner * INV_ROOT_TWO))
    acted = (inner * phi).astype(BF)
    slope = phi + inner * jnp.exp(-0.5 * inner * inner) * INV_ROOT_TWO_PI
    down_part = mm(acted, wd).astype(BF)

    output, d_two, sums_two, d_two_all = norm_two_step(
        down_part, hidden, bd, gtwo, stwo, out_cotangent
    )
    d_inner = mm_nt(d_two_all, wd) * slope
    g_bias_inner = jnp.sum(d_inner, axis=0)
    d_inner_b = d_inner.astype(BF)
    hid_part = mm_nt(d_inner_b, wi).astype(BF)
    g_wd = mm_tn(acted, d_two_all).astype(BF).reshape(S, dv, V)
    g_wi = mm_tn(hidden_all, d_inner_b).astype(BF).reshape(S, ds, V)
    g_mlp = lax.psum_scatter(
        jnp.concatenate([g_wi, g_wd], 1), "shard", scatter_dimension=0, tiled=True
    )[0]

    d_one, sums_one, d_one_all = back_one_step(hid_part, d_two, normed_one, rstd_one, gone)
    g_wo = mm_tn(context, d_one_all).astype(BF)
    g_wo = lax.all_to_all(g_wo, "rep", split_axis=1, concat_axis=0, tiled=True)
    d_context = mm_nt(d_one_all, wo).astype(BF).reshape(shape4)
    d_probs = ein("bqhe,bkhe->bhqk", d_context, valued)
    delta = jnp.sum(probs * d_probs, axis=-1, keepdims=True)
    d_scores = (probs * (d_probs - delta) * 0.125).astype(BF)
    d_query = ein("bhqk,bkhe->bqhe", d_scores, keyed).reshape(N, dr)
    d_keyed = ein("bhqk,bqhe->bkhe", d_scores, query).reshape(N, dr)
    d_valued = ein("bhqk,bqhe->bkhe", probs_b, d_context).reshape(N, dr)
    g_bias_query = jnp.sum(d_query, axis=0)
    g_bias_value = jnp.sum(d_valued, axis=0)
    d_qkv = jnp.concatenate([d_query.astype(BF), d_keyed.astype(BF), d_valued.astype(BF)], 1)
    in_part = mm_nt(d_qkv, wqkv).astype(BF)

    def placed(v):
        return lax.dynamic_update_slice(jnp.zeros((D,), F32), v, (r * dr,)).reshape(S, ds)

    g_small = jnp.concatenate(
        [
            placed(g_bias_query),
            placed(g_bias_value),
            sums_one[0].reshape(S, ds),
            sums_one[1].reshape(S, ds),
            sums_one[2].reshape(S, ds),
            sums_two[0].reshape(S, ds),
            sums_two[1].reshape(S, ds),
            sums_two[2].reshape(S, ds),
            g_bias_inner.reshape(S, fr),
        ],
        1,
    ).astype(BF)
    n_g = g_small.shape[1]
    g_small = jnp.pad(g_small, ((0, 0), (0, PAD * W - n_g))).reshape(S, PAD, W)
    g_pack = jnp.concatenate([mm_tn(x_all, d_qkv).astype(BF), g_wo], 1).reshape(S, ds, W)
    g_pack = jnp.concatenate([g_pack, g_small], 1)
    g_pack = lax.psum_scatter(g_pack, "shard", scatter_dimension=0, tiled=True)[0]

    grad_input = input_step(in_part, d_one)

    mlps = gather_kernel(g_mlp, R, 5).reshape(R, ds + dv, V).astype(F32)
    wd_out = mlps[:, ds:].reshape(R * fr, D)
    wi_out = mlps[:, :ds].reshape(R, ds, S, fr).transpose(1, 2, 0, 3).reshape(ds, S * R * fr)
    packs = gather_kernel(g_pack, R, 6).reshape(R, ds + PAD, W).astype(F32)
    main = packs[:, :ds].reshape(R, ds, 4, dr).transpose(2, 1, 0, 3).reshape(4, ds, D)
    tail = packs[:, ds:].reshape(R, PAD * W)
    summed = jnp.sum(tail[:, : 8 * ds], axis=0)
    gbq, gbv, gbo, ggone, gsone, gbd, ggtwo, gstwo = (
        summed[i * ds : (i + 1) * ds] for i in range(8)
    )
    gbi = tail[:, 8 * ds : n_g].reshape(fs)
    return (
        output,
        grad_input,
        main[0],
        main[1],
        main[2],
        main[3],
        gbq,
        gbv,
        gbo,
        ggone,
        gsone,
        wi_out,
        gbi,
        wd_out,
        gbd,
        ggtwo,
        gstwo,
    )


def solution(mesh):
    tokens = P(("shard", "rep"), None)
    mat = P("shard", None)
    vec = P("shard")
    params = (mat, mat, mat, mat, vec, vec, vec, vec, vec, mat, vec, mat, vec, vec, vec)
    return jax.shard_map(
        body,
        mesh=mesh,
        in_specs=(tokens, tokens) + params,
        out_specs=(tokens, tokens) + params,
        check_vma=False,
    )
```
